1024 devices in a mesh: ctx: 128 (over z, x), tp: 8 (over y, core).
Axes of the slice: x: 4, y: 4, z: 32, core: 2. Of those that a mesh axis runs over, the one named last changes fastest.
Arguments:
- q_proj: bfloat16 [16384, 8192], P('ctx', 'tp'), may hold values from -110 to 110, as said below
- k_proj: bfloat16 [16384, 8192], P('ctx', 'tp'), may hold values from -6 to 6
- v_proj: bfloat16 [16384, 8192], P('ctx', 'tp'), may hold values from -6 to 6
- cotangent: bfloat16 [16384, 8192], P('ctx', 'tp'), may hold values from -6 to 6
- filters: float32 [128, 8192], P(None, 'tp'), may hold values from -0.5 to 0.5
- gain: float32 [8192], P('tp'), may hold values from 0.5 to 1.5
Outputs:
- grad_q: bfloat16 [16384, 8192], P('ctx', 'tp')
- grad_k: bfloat16 [16384, 8192], P('ctx', 'tp')
- grad_v: bfloat16 [16384, 8192], P('ctx', 'tp')
- grad_filters: float32 [128, 8192], P(None, 'tp')
- grad_gain: float32 [8192], P('tp')
The draws below stay inside these ranges and needn't reach their ends.
Inputs may be any that keep to these rules, and one draw needn't show every extreme that they name: q_proj has entries of varying magnitude.
All inputs are finite; a program needn't handle non-finite values.
Results may differ from the reference program's by a relative error of at most 0.0049.
Values may be sent and summed in bfloat16 or wider, within the bound.
No kernel may reach another device: no remote copies, remote signals or barrier semaphores. Data moves between devices by JAX's collectives and lax.ppermute only.
A program may use at most 32 MiB of HBM per device.

```python
import math
import jax
import jax.numpy as jnp
from jax import lax

D = 8192
TAPS = 128
TOKENS = 16384


def draw_q_proj(key, part):
    key_base, key_rows, key_cols = jax.random.split(jax.random.fold_in(key, 11), 3)
    base = jax.random.truncated_normal(key_base, -6.0, 6.0, (TOKENS, D), jnp.float32)
    span = math.log(10.0)
    row_scale = jnp.exp(span * (jax.random.uniform(key_rows, (TOKENS, 1), jnp.float32) - 0.5))
    ramp = jnp.arange(D, dtype=jnp.float32)[None, :] / D - 0.5
    col_scale = jnp.exp(span * (jax.random.uniform(key_cols, (1, D), jnp.float32) - 0.5) + math.log(3.0) * ramp)
    return (base * row_scale * col_scale).astype(jnp.bfloat16)


def level_of(own_key, shape, pieces, smallest, high):
    factor_of = 1.0
    for dim, shards_of in pieces:
        heights = jax.random.uniform(jax.random.fold_in(jax.random.fold_in(own_key, 6), dim), (shards_of,), jnp.float32, smallest / len(pieces), high / len(pieces))
        factor_of = factor_of * jnp.repeat(jnp.exp(heights), shape[dim] // shards_of).reshape((-1,) + (1,) * (len(shape) - 1 - dim))
    return factor_of


def centred(key, shape, deviation, most, pieces=(), kind=jnp.bfloat16):
    drawn = jax.random.normal(key, shape, jnp.float32) * deviation
    if len(pieces) > 0:
        drawn = level_of(key, shape, pieces, -0.22, 0.18) * drawn
    return jnp.clip(drawn, min=-most, max=most).astype(kind)


def setup_inputs(seed: int = 0) -> dict:
    seeds = jax.random.split(jax.random.key(seed), 7)
    q_proj = draw_q_proj(jax.random.fold_in(seeds[6], 71), 0)
    k_proj = centred(seeds[1], (TOKENS, D), 1.0, 6.0, ((0, 128), (1, 8)))
    v_proj = centred(seeds[2], (TOKENS, D), 1.0, 6.0, ((0, 128), (1, 8)))
    cotangent = centred(seeds[3], (TOKENS, D), 1.0, 6.0, ((0, 128), (1, 8)))
    filters = centred(seeds[4], (TAPS, D), TAPS ** -0.5, 0.5, ((1, 8),), jnp.float32)
    gain = jnp.clip(0.5 + 1.0 * jax.random.uniform(seeds[5], (D,), jnp.float32) ** level_of(seeds[5], (D,), ((0, 8),), -0.2, 0.2), 0.5, 1.5)
    return dict(q_proj=q_proj, k_proj=k_proj, v_proj=v_proj, cotangent=cotangent, filters=filters, gain=gain)


epsilon = 1e-06

def causal_sum(extended, kernel, out_rows):
    rim_rows = kernel.shape[0] - 1

    def add_tap(index, total):
        tap = index.astype(jnp.int32)
        weights = lax.dynamic_index_in_dim(kernel, tap, 0, False)
        start = (rim_rows - tap).astype(jnp.int32)
        return total + weights[None, :] * lax.dynamic_slice_in_dim(extended, start, out_rows, 0)
    empty = jnp.zeros((out_rows, extended.shape[1]), jnp.float32)
    return lax.fori_loop(0, kernel.shape[0], add_tap, empty)

def anticausal_sum(extended, kernel, out_rows):

    def add_tap(index, total):
        tap = index.astype(jnp.int32)
        weights = lax.dynamic_index_in_dim(kernel, tap, 0, False)
        return total + weights[None, :] * lax.dynamic_slice_in_dim(extended, tap, out_rows, 0)
    empty = jnp.zeros((out_rows, extended.shape[1]), jnp.float32)
    return lax.fori_loop(0, kernel.shape[0], add_tap, empty)

def reference(q_proj, k_proj, v_proj, cotangent, filters, gain):
    block_width = math.gcd(D, 1024)
    block_count = D // block_width
    rim_rows = TAPS - 1
    indices = jnp.arange(block_count, dtype=jnp.int32)
    tap_ids = jnp.arange(TAPS, dtype=jnp.int32)

    def columns(array, block):
        return lax.dynamic_slice_in_dim(array, (block * block_width).astype(jnp.int32), block_width, array.ndim - 1)

    def mixed_ext(block):
        mixed = (columns(k_proj, block).astype(jnp.float32) * columns(v_proj, block).astype(jnp.float32)).astype(jnp.bfloat16)
        return jnp.concatenate([jnp.zeros((rim_rows, block_width), jnp.float32), mixed.astype(jnp.float32)], 0)

    def first_pass(block):
        conv_fwd = causal_sum(mixed_ext(block), columns(filters, block), TOKENS)
        product = columns(q_proj, block).astype(jnp.float32) * conv_fwd
        weighted = columns(gain, block) * columns(cotangent, block).astype(jnp.float32)
        return (lax.optimization_barrier(jnp.sum(product * product, 1)), lax.optimization_barrier(jnp.sum(weighted * product, 1)), conv_fwd)
    squares, crosses, convs = lax.map(first_pass, indices)
    rms = jnp.sqrt(lax.optimization_barrier(jnp.sum(squares, 0)) / D + epsilon)[:, None]
    cross = lax.optimization_barrier(jnp.sum(crosses, 0))[:, None]

    def second_pass(item):
        block, conv_fwd = item
        query = columns(q_proj, block).astype(jnp.float32)
        cot_block = columns(cotangent, block).astype(jnp.float32)
        product = query * conv_fwd
        grad_product = columns(gain, block) * cot_block / rms - product * cross / (D * rms ** 3)
        grad_conv = (query * grad_product).astype(jnp.bfloat16)
        grad_q = (grad_product * conv_fwd).astype(jnp.bfloat16)
        conv_float = grad_conv.astype(jnp.float32)
        conv_ext = jnp.concatenate([conv_float, jnp.zeros((rim_rows, block_width), jnp.float32)], 0)
        grad_mixed = anticausal_sum(conv_ext, columns(filters, block), TOKENS)
        grad_k = (grad_mixed * columns(v_proj, block).astype(jnp.float32)).astype(jnp.bfloat16)
        grad_v = (grad_mixed * columns(k_proj, block).astype(jnp.float32)).astype(jnp.bfloat16)
        extended = mixed_ext(block)

        def tap_grad(tap):
            start = (rim_rows - tap).astype(jnp.int32)
            return lax.optimization_barrier(jnp.sum(conv_float * lax.dynamic_slice_in_dim(extended, start, TOKENS, 0), 0))
        grad_filters = lax.map(tap_grad, tap_ids)
        grad_gain = lax.optimization_barrier(jnp.sum(cot_block * product / rms, 0))
        return (grad_q, grad_k, grad_v, grad_filters, grad_gain)
    grad_q, grad_k, grad_v, grad_filters, grad_gain = lax.map(second_pass, (indices, convs))

    def unblock(stacked):
        return jnp.transpose(stacked, (1, 0, 2)).reshape(stacked.shape[1], D)
    return (unblock(grad_q), unblock(grad_k), unblock(grad_v), unblock(grad_filters), grad_gain.reshape(D))
```

```python
import jax
import jax.numpy as jnp
from jax import lax
from jax.sharding import Mesh, PartitionSpec as P

D = 8192
CTX = ("zh", "zl", "x")
NEAR = ("zl", "x")
FAR = "zh"

epsilon = 1e-06


def passed_along(value, by):
    length = lax.axis_size(CTX)
    pairs = [(i, i + by) for i in range(length) if 0 <= i + by < length]
    return lax.ppermute(value, CTX, pairs)


def shared(value, axes):
    size = lax.axis_size(axes)
    copies = jnp.broadcast_to(value[None], (size, *value.shape))
    return lax.all_to_all(copies, axes, 0, 0)


def depthwise(signal, kernel):
    return lax.conv_general_dilated(
        signal[None],
        kernel[:, None, :],
        (1,),
        "VALID",
        dimension_numbers=("NWC", "WIO", "NWC"),
        feature_group_count=signal.shape[1],
        precision=lax.Precision.HIGHEST,
    )[0]


def token_sums(local_filters, local_gain):
    taps, width = local_filters.shape
    near = lax.axis_size(NEAR)
    rows = taps // near
    parts = local_gain.reshape(width // 128, 1, 128)
    parts = jnp.pad(parts, ((0, near - width // 128), (0, rows - 1), (0, 0))).reshape(taps, 128)
    block = jnp.concatenate([local_filters, parts], 1).reshape(near, rows, width + 128)
    own = lax.all_to_all(block.astype(jnp.bfloat16), NEAR, 0, 0)
    own = jnp.sum(own.astype(jnp.float32), 0)
    own = shared(own.astype(jnp.bfloat16), FAR)
    own = jnp.sum(own.astype(jnp.float32), 0)
    whole = shared(own.astype(jnp.bfloat16), NEAR).astype(jnp.float32)
    grad_filters = whole[:, :, :width].reshape(taps, width)
    grad_gain = whole[: width // 128, 0, width:].reshape(width)
    return grad_filters, grad_gain


def shards(q_proj, k_proj, v_proj, cotangent, filters, gain):
    tap_count = filters.shape[0]
    rim_rows = tap_count - 1
    tok_rows = q_proj.shape[0]
    mixed = (k_proj.astype(jnp.float32) * v_proj.astype(jnp.float32)).astype(jnp.bfloat16)
    earlier = passed_along(mixed, 1)
    mixed_ext = jnp.concatenate([earlier, mixed], 0).astype(jnp.float32)[tok_rows - rim_rows :]
    flipped = filters[::-1]
    conv_fwd = depthwise(mixed_ext, flipped)
    query_f32 = q_proj.astype(jnp.float32)
    cot_f32 = cotangent.astype(jnp.float32)
    product = query_f32 * conv_fwd
    weighted = gain * cot_f32
    sums = jnp.stack([jnp.sum(product * product, 1), jnp.sum(weighted * product, 1)])
    sums = jnp.pad(sums, ((0, 6), (0, 0)))
    sum_squares, sum_cross = jnp.sum(shared(sums, "tp"), 0)[:2]
    rms = jnp.sqrt(sum_squares / D + epsilon)[:, None]
    cross = sum_cross[:, None]
    grad_product = weighted / rms - product * cross / (D * rms**3)
    grad_conv = (query_f32 * grad_product).astype(jnp.bfloat16)
    later = passed_along(grad_conv, -1)
    conv_ext = jnp.concatenate([grad_conv, later[:rim_rows]], 0)
    grad_q = (grad_product * conv_fwd).astype(jnp.bfloat16)
    local_filters = depthwise(mixed_ext, grad_conv.astype(jnp.float32))[::-1]
    local_gain = jnp.sum(cot_f32 * product / rms, 0)
    grad_filters, grad_gain = token_sums(local_filters, local_gain)
    grad_mixed = depthwise(conv_ext.astype(jnp.float32), filters)
    grad_k = (grad_mixed * v_proj.astype(jnp.float32)).astype(jnp.bfloat16)
    grad_v = (grad_mixed * k_proj.astype(jnp.float32)).astype(jnp.bfloat16)
    return (grad_q, grad_k, grad_v, grad_filters, grad_gain)


def solution(mesh):
    cube = 4
    far = mesh.devices.shape[0] // (cube * cube)
    split = Mesh(mesh.devices.reshape(far, cube, cube, -1), (*CTX, "tp"))
    rows = P(CTX, "tp")
    in_specs = (rows, rows, rows, rows, P(None, "tp"), P("tp"))
    out_specs = (rows, rows, rows, P(None, "tp"), P("tp"))
    return jax.shard_map(shards, mesh=split, in_specs=in_specs, out_specs=out_specs, check_vma=False)
```

```python
import jax
import jax.numpy as jnp
from jax import lax
from jax.experimental import pallas as pl
from jax.experimental.pallas import tpu as pltpu
from jax.sharding import Mesh, PartitionSpec as P

D = 8192
CTX = ("zh", "zl", "x")
NEAR = ("zl", "x")
FAR = "zh"
LANES = 128
SUB = 8
VMEM_BYTES = 8 << 20

epsilon = 1e-06
f32 = jnp.float32
bf16 = jnp.bfloat16


def passed_along(value, by):
    length = lax.axis_size(CTX)
    pairs = [(i, i + by) for i in range(length) if 0 <= i + by < length]
    return lax.ppermute(value, CTX, pairs)


def shared(value, axes):
    size = lax.axis_size(axes)
    copies = jnp.broadcast_to(value[None], (size, *value.shape))
    return lax.all_to_all(copies, axes, 0, 0)


def call(kernel, outs, *operands, scratch=(), name, flops):
    in_vmem = pl.BlockSpec(memory_space=pltpu.VMEM)
    moved = sum(x.size * x.dtype.itemsize for x in (*operands, *outs))
    return pl.pallas_call(
        kernel,
        out_shape=outs,
        in_specs=[in_vmem] * len(operands),
        out_specs=tuple(in_vmem for _ in outs),
        scratch_shapes=list(scratch),
        name=name,
        compiler_params=pltpu.CompilerParams(vmem_limit_bytes=VMEM_BYTES),
        cost_estimate=pl.CostEstimate(flops=flops, bytes_accessed=moved, transcendentals=0),
    )(*operands)


def struct(shape, dtype):
    return jax.ShapeDtypeStruct(shape, dtype)


def over_tiles(width, body):
    def step(tile, carry):
        body(tile, pl.ds(pl.multiple_of(tile * LANES, LANES), LANES))
        return carry

    lax.fori_loop(0, width // LANES, step, 0)


def blocks(value):
    return [value[SUB * i : SUB * i + SUB] for i in range(value.shape[0] // SUB)]


def fill(window, at, value):
    window[pl.ds(at, value.shape[0]), :] = value.astype(f32)


def own_kernel(mixed, filters, conv, window):
    rows, width = mixed.shape
    count = rows // SUB
    window[pl.ds(0, SUB), :] = jnp.zeros((SUB, LANES), f32)

    def tile(_, lanes):
        fill(window, SUB, mixed[:, lanes])
        total = [None] * count
        for shift in range(SUB):
            slid = [window[pl.ds(SUB + SUB * i - shift, SUB), :] for i in range(count)]
            for step in range(count):
                weight = filters[pl.ds(SUB * step + shift, 1), lanes]
                for i in range(step, count):
                    term = weight * slid[i - step]
                    total[i] = term if total[i] is None else total[i] + term
        for i in range(count):
            conv[pl.ds(SUB * i, SUB), lanes] = total[i]

    over_tiles(width, tile)


def rim_kernel(own, earlier, filters, query, cot, gain, conv, sums, window, squares, crosses):
    rows, width = own.shape
    count = rows // SUB
    window[pl.ds(rows, SUB), :] = jnp.zeros((SUB, LANES), f32)
    squares[...] = jnp.zeros(squares.shape, f32)
    crosses[...] = jnp.zeros(crosses.shape, f32)

    def tile(_, lanes):
        fill(window, 0, earlier[:, lanes])
        total = [own[pl.ds(SUB * i, SUB), lanes] for i in range(count)]
        for shift in range(SUB):
            slid = [window[pl.ds(rows - SUB * i - shift, SUB), :] for i in range(count)]
            for step in range(count):
                weight = filters[pl.ds(SUB * step + shift, 1), lanes]
                for i in range(step + 1):
                    total[i] = total[i] + weight * slid[step - i]
        for i in range(count):
            at = pl.ds(SUB * i, SUB)
            conv[at, lanes] = total[i]
        whole = conv[:, lanes]
        product = query[:, lanes].astype(f32) * whole
        weighted = gain[:, lanes] * cot[:, lanes].astype(f32)
        squares[...] += product * product
        crosses[...] += weighted * product

    over_tiles(width, tile)
    square = jnp.sum(squares[...].T, 0, keepdims=True)
    cross = jnp.sum(crosses[...].T, 0, keepdims=True)
    first = lax.broadcasted_iota(jnp.int32, sums.shape[1:], 0) == 0
    both = jnp.where(first, square, cross)
    for i in range(sums.shape[0]):
        sums[i] = both


def gathered(parts):
    row = lax.broadcasted_iota(jnp.int32, (SUB, LANES), 0)
    half = 1
    while half < SUB:
        low = (row & half) == 0
        parts = [
            jnp.where(low, a, b) + pltpu.roll(jnp.where(low, b, a), half, 0)
            for a, b in zip(parts[::2], parts[1::2])
        ]
        half *= 2
    return parts[0]


def grads_kernel(
    sums, conv, query, cot, gain, earlier, mixed, grad_conv, grad_q, block, window, inverse, pull, partial
):
    rows, width = conv.shape
    count = rows // SUB
    both = jnp.sum(sums[...], 0)
    rms = jnp.sqrt(both[0:1] / D + epsilon)
    inverse[...] = jnp.broadcast_to(1.0 / rms, (LANES, rows)).T
    pull[...] = jnp.broadcast_to(both[1:2] / (D * (rms * rms * rms)), (LANES, rows)).T
    block[:, width:] = jnp.zeros((rows, LANES), bf16)

    def tile(index, lanes):
        whole = conv[:, lanes]
        query_f32 = query[:, lanes].astype(f32)
        cot_f32 = cot[:, lanes].astype(f32)
        product = query_f32 * whole
        grad_product = gain[:, lanes] * cot_f32 * inverse[...] - product * pull[...]
        rounded = (query_f32 * grad_product).astype(bf16)
        grad_conv[:, lanes] = rounded
        grad_q[:, lanes] = (grad_product * whole).astype(bf16)
        gains = jnp.sum((cot_f32 * product * inverse[...]).reshape(count, SUB, LANES), 0)
        block[pl.ds(pl.multiple_of(index * SUB, SUB), SUB), width:] = gains.astype(bf16)
        fill(window, 0, earlier[:, lanes])
        fill(window, rows, mixed[:, lanes])
        ours = blocks(rounded.astype(f32))
        for shift in range(SUB):
            slid = [window[pl.ds(SUB * (i + 1) - shift, SUB), :] for i in range(2 * count - 1)]
            for step in range(count):
                terms = [ours[i] * slid[count - 1 + i - step] for i in range(count)]
                while len(terms) > 1:
                    terms = [a + b for a, b in zip(terms[::2], terms[1::2])]
                partial[SUB * step + shift] = terms[0]
        for step in range(0, count, 2):
            pair = [gathered([partial[SUB * s + i] for i in range(SUB)]) for s in (step, step + 1)]
            block[pl.ds(SUB * step, 2 * SUB), lanes] = jnp.concatenate(pair, 0).astype(bf16)

    over_tiles(width, tile)


def back_kernel(grad_conv, later, filters, k_proj, v_proj, grad_k, grad_v, window):
    rows, width = grad_conv.shape
    count = rows // SUB

    def tile(_, lanes):
        fill(window, 0, grad_conv[:, lanes])
        fill(window, rows, later[:, lanes])
        total = [jnp.zeros((SUB, LANES), f32)] * count
        for shift in range(SUB):
            slid = [window[pl.ds(SUB * i + shift, SUB), :] for i in range(2 * count - 1)]
            for step in range(count):
                weight = filters[pl.ds(SUB * step + shift, 1), lanes]
                for i in range(count):
                    total[i] = total[i] + weight * slid[i + step]
        grad_mixed = jnp.concatenate(total, 0)
        grad_k[:, lanes] = (grad_mixed * v_proj[:, lanes].astype(f32)).astype(bf16)
        grad_v[:, lanes] = (grad_mixed * k_proj[:, lanes].astype(f32)).astype(bf16)

    over_tiles(width, tile)


def final_kernel(whole, grad_filters, grad_gain):
    width = grad_filters.shape[1]
    grad_filters[...] = whole[:, :width].astype(f32)
    for i in range(width // LANES):
        part = whole[pl.ds(SUB * i, SUB), width:].astype(f32)
        grad_gain[pl.ds(i, 1), :] = jnp.sum(part, 0, keepdims=True)


def shards(q_proj, k_proj, v_proj, cotangent, filters, gain):
    rows, width = q_proj.shape
    macs = 2 * filters.shape[0] * rows * width
    tile = pltpu.VMEM((rows, LANES), f32)
    short = pltpu.VMEM((rows + SUB, LANES), f32)
    long = pltpu.VMEM((2 * rows, LANES), f32)
    gain = gain.reshape(1, width)
    mixed = (k_proj.astype(f32) * v_proj.astype(f32)).astype(bf16)
    earlier = passed_along(mixed, 1)
    (own,) = call(
        own_kernel, (struct((rows, width), f32),), mixed, filters, scratch=(short,), name="own", flops=macs // 2
    )
    members = lax.axis_size("tp")
    conv, sums = call(
        rim_kernel,
        (struct((rows, width), f32), struct((members, SUB, rows), f32)),
        own,
        earlier,
        filters,
        q_proj,
        cotangent,
        gain,
        scratch=(short, tile, tile),
        name="rim",
        flops=macs // 2,
    )
    sums = lax.all_to_all(sums, "tp", 0, 0)
    grad_conv, grad_q, block = call(
        grads_kernel,
        (struct((rows, width), bf16), struct((rows, width), bf16), struct((rows, width + LANES), bf16)),
        sums,
        conv,
        q_proj,
        cotangent,
        gain,
        earlier,
        mixed,
        scratch=(long, tile, tile, pltpu.VMEM((rows, SUB, LANES), f32)),
        name="grads",
        flops=macs,
    )
    near = lax.axis_size(NEAR)
    block = block.reshape(near, rows // near, width + LANES)
    block = lax.all_to_all(block, NEAR, 0, 0)
    block = jnp.sum(block.astype(f32), 0).astype(bf16)
    block, grad_conv = lax.optimization_barrier((block, grad_conv))
    block = shared(block, FAR)
    later = passed_along(grad_conv, -1)
    grad_k, grad_v = call(
        back_kernel,
        (struct((rows, width), bf16), struct((rows, width), bf16)),
        grad_conv,
        later,
        filters,
        k_proj,
        v_proj,
        scratch=(long,),
        name="back",
        flops=macs,
    )
    block = jnp.sum(block.astype(f32), 0).astype(bf16)
    block, grad_k = lax.optimization_barrier((block, grad_k))
    whole = shared(block, NEAR).reshape(rows, width + LANES)
    grad_filters, grad_gain = call(
        final_kernel,
        (struct((rows, width), f32), struct((width // LANES, LANES), f32)),
        whole,
        name="final",
        flops=0,
    )
    return (grad_q, grad_k, grad_v, grad_filters, grad_gain.reshape(width))


def solution(mesh):
    cube = 4
    far = mesh.devices.shape[0] // (cube * cube)
    split = Mesh(mesh.devices.reshape(far, cube, cube, -1), (*CTX, "tp"))
    rows = P(CTX, "tp")
    in_specs = (rows, rows, rows, rows, P(None, "tp"), P("tp"))
    out_specs = (rows, rows, rows, P(None, "tp"), P("tp"))
    return jax.shard_map(shards, mesh=split, in_specs=in_specs, out_specs=out_specs, check_vma=False)
```

```python
import jax
import jax.numpy as jnp
from jax import lax
from jax.experimental import pallas as pl
from jax.experimental.pallas import tpu as pltpu
from jax.sharding import Mesh, PartitionSpec as P

D = 8192
CTX = ("zh", "zl", "x")
NEAR = ("zl", "x")
FAR = "zh"
LANES = 128
SUB = 8
VMEM_BYTES = 8 << 20

epsilon = 1e-06
f32 = jnp.float32
bf16 = jnp.bfloat16


def passed_along(value, by):
    length = lax.axis_size(CTX)
    pairs = [(i, i + by) for i in range(length) if 0 <= i + by < length]
    return lax.ppermute(value, CTX, pairs)


def shared(value, axes):
    size = lax.axis_size(axes)
    copies = jnp.broadcast_to(value[None], (size, *value.shape))
    return lax.all_to_all(copies, axes, 0, 0)


def call(kernel, outs, *operands, scratch=(), name, flops):
    in_vmem = pl.BlockSpec(memory_space=pltpu.VMEM)
    moved = sum(x.size * x.dtype.itemsize for x in (*operands, *outs))
    return pl.pallas_call(
        kernel,
        out_shape=outs,
        in_specs=[in_vmem] * len(operands),
        out_specs=tuple(in_vmem for _ in outs),
        scratch_shapes=list(scratch),
        name=name,
        compiler_params=pltpu.CompilerParams(vmem_limit_bytes=VMEM_BYTES),
        cost_estimate=pl.CostEstimate(flops=flops, bytes_accessed=moved, transcendentals=0),
    )(*operands)


def struct(shape, dtype):
    return jax.ShapeDtypeStruct(shape, dtype)


def over_tiles(width, body):
    def step(tile, carry):
        body(tile, pl.ds(pl.multiple_of(tile * LANES, LANES), LANES))
        return carry

    lax.fori_loop(0, width // LANES, step, 0)


def blocks(value):
    return [value[SUB * i : SUB * i + SUB] for i in range(value.shape[0] // SUB)]


def fill(window, at, value):
    window[pl.ds(at, value.shape[0]), :] = value.astype(f32)


def own_kernel(mixed, filters, conv, window):
    rows, width = mixed.shape
    count = rows // SUB
    window[pl.ds(0, SUB), :] = jnp.zeros((SUB, LANES), f32)

    def tile(_, lanes):
        fill(window, SUB, mixed[:, lanes])
        total = [None] * count
        for shift in range(SUB):
            slid = [window[pl.ds(SUB + SUB * i - shift, SUB), :] for i in range(count)]
            for step in range(count):
                weight = filters[pl.ds(SUB * step + shift, 1), lanes]
                for i in range(step, count):
                    term = weight * slid[i - step]
                    total[i] = term if total[i] is None else total[i] + term
        for i in range(count):
            conv[pl.ds(SUB * i, SUB), lanes] = total[i]

    over_tiles(width, tile)


def rim_kernel(own, earlier, filters, query, cot, gain, conv, sums, window, squares, crosses):
    rows, width = own.shape
    count = rows // SUB
    window[pl.ds(rows, SUB), :] = jnp.zeros((SUB, LANES), f32)
    squares[...] = jnp.zeros(squares.shape, f32)
    crosses[...] = jnp.zeros(crosses.shape, f32)

    def tile(_, lanes):
        fill(window, 0, earlier[:, lanes])
        total = [own[pl.ds(SUB * i, SUB), lanes] for i in range(count)]
        for shift in range(SUB):
            slid = [window[pl.ds(rows - SUB * i - shift, SUB), :] for i in range(count)]
            for step in range(count):
                weight = filters[pl.ds(SUB * step + shift, 1), lanes]
                for i in range(step + 1):
                    total[i] = total[i] + weight * slid[step - i]
        for i in range(count):
            at = pl.ds(SUB * i, SUB)
            conv[at, lanes] = total[i]
        whole = conv[:, lanes]
        product = query[:, lanes].astype(f32) * whole
        weighted = gain[:, lanes] * cot[:, lanes].astype(f32)
        squares[...] += product * product
        crosses[...] += weighted * product

    over_tiles(width, tile)
    square = jnp.sum(squares[...].T, 0, keepdims=True)
    cross = jnp.sum(crosses[...].T, 0, keepdims=True)
    first = lax.broadcasted_iota(jnp.int32, sums.shape[1:], 0) == 0
    both = jnp.where(first, square, cross)
    for i in range(sums.shape[0]):
        sums[i] = both


def gathered(parts):
    row = lax.broadcasted_iota(jnp.int32, (SUB, LANES), 0)
    half = 1
    while half < SUB:
        low = (row & half) == 0
        parts = [
            jnp.where(low, a, b) + pltpu.roll(jnp.where(low, b, a), half, 0)
            for a, b in zip(parts[::2], parts[1::2])
        ]
        half *= 2
    return parts[0]


def grads_kernel(sums, conv, query, cot, gain, grad_conv, grad_q, gains, inverse, pull):
    rows, width = conv.shape
    both = jnp.sum(sums[...], 0)
    rms = jnp.sqrt(both[0:1] / D + epsilon)
    inverse[...] = jnp.broadcast_to(1.0 / rms, (LANES, rows)).T
    pull[...] = jnp.broadcast_to(both[1:2] / (D * (rms * rms * rms)), (LANES, rows)).T

    def tile(index, lanes):
        whole = conv[:, lanes]
        query_f32 = query[:, lanes].astype(f32)
        cot_f32 = cot[:, lanes].astype(f32)
        product = query_f32 * whole
        grad_product = gain[:, lanes] * cot_f32 * inverse[...] - product * pull[...]
        grad_conv[:, lanes] = (query_f32 * grad_product).astype(bf16)
        grad_q[:, lanes] = (grad_product * whole).astype(bf16)
        parts = (cot_f32 * product * inverse[...]).reshape(rows // SUB, SUB, LANES)
        gains[pl.ds(pl.multiple_of(index * SUB, SUB), SUB), :] = jnp.sum(parts, 0).astype(bf16)

    over_tiles(width, tile)


def taps_kernel(grad_conv, gains, earlier, mixed, block, window, partial):
    rows, width = grad_conv.shape
    count = rows // SUB
    block[:, width:] = jnp.zeros((rows, LANES), bf16)
    block[pl.ds(0, gains.shape[0]), width:] = gains[...]

    def tile(_, lanes):
        fill(window, 0, earlier[:, lanes])
        fill(window, rows, mixed[:, lanes])
        ours = blocks(grad_conv[:, lanes].astype(f32))
        for shift in range(SUB):
            slid = [window[pl.ds(SUB * (i + 1) - shift, SUB), :] for i in range(2 * count - 1)]
            for step in range(count):
                terms = [ours[i] * slid[count - 1 + i - step] for i in range(count)]
                while len(terms) > 1:
                    terms = [a + b for a, b in zip(terms[::2], terms[1::2])]
                partial[SUB * step + shift] = terms[0]
        for step in range(0, count, 2):
            pair = [gathered([partial[SUB * s + i] for i in range(SUB)]) for s in (step, step + 1)]
            block[pl.ds(SUB * step, 2 * SUB), lanes] = jnp.concatenate(pair, 0).astype(bf16)

    over_tiles(width, tile)


def back_kernel(grad_conv, later, filters, k_proj, v_proj, grad_k, grad_v, window):
    rows, width = grad_conv.shape
    count = rows // SUB

    def tile(_, lanes):
        fill(window, 0, grad_conv[:, lanes])
        fill(window, rows, later[:, lanes])
        total = [jnp.zeros((SUB, LANES), f32)] * count
        for shift in range(SUB):
            slid = [window[pl.ds(SUB * i + shift, SUB), :] for i in range(2 * count - 1)]
            for step in range(count):
                weight = filters[pl.ds(SUB * step + shift, 1), lanes]
                for i in range(count):
                    total[i] = total[i] + weight * slid[i + step]
        grad_mixed = jnp.concatenate(total, 0)
        grad_k[:, lanes] = (grad_mixed * v_proj[:, lanes].astype(f32)).astype(bf16)
        grad_v[:, lanes] = (grad_mixed * k_proj[:, lanes].astype(f32)).astype(bf16)

    over_tiles(width, tile)


def final_kernel(whole, grad_filters, grad_gain):
    width = grad_filters.shape[1]
    grad_filters[...] = whole[:, :width].astype(f32)
    for i in range(width // LANES):
        part = whole[pl.ds(SUB * i, SUB), width:].astype(f32)
        grad_gain[pl.ds(i, 1), :] = jnp.sum(part, 0, keepdims=True)


def shards(q_proj, k_proj, v_proj, cotangent, filters, gain):
    rows, width = q_proj.shape
    macs = 2 * filters.shape[0] * rows * width
    tile = pltpu.VMEM((rows, LANES), f32)
    short = pltpu.VMEM((rows + SUB, LANES), f32)
    long = pltpu.VMEM((2 * rows, LANES), f32)
    gain = gain.reshape(1, width)
    mixed = (k_proj.astype(f32) * v_proj.astype(f32)).astype(bf16)
    earlier = passed_along(mixed, 1)
    (own,) = call(
        own_kernel, (struct((rows, width), f32),), mixed, filters, scratch=(short,), name="own", flops=macs // 2
    )
    members = lax.axis_size("tp")
    conv, sums = call(
        rim_kernel,
        (struct((rows, width), f32), struct((members, SUB, rows), f32)),
        own,
        earlier,
        filters,
        q_proj,
        cotangent,
        gain,
        scratch=(short, tile, tile),
        name="rim",
        flops=macs // 2,
    )
    sums = lax.all_to_all(sums, "tp", 0, 0)
    grad_conv, grad_q, gains = call(
        grads_kernel,
        (struct((rows, width), bf16), struct((rows, width), bf16), struct((width // LANES * SUB, LANES), bf16)),
        sums,
        conv,
        q_proj,
        cotangent,
        gain,
        scratch=(tile, tile),
        name="grads",
        flops=rows * width * 12,
    )
    later = passed_along(grad_conv, -1)
    (block,) = call(
        taps_kernel,
        (struct((rows, width + LANES), bf16),),
        grad_conv,
        gains,
        earlier,
        mixed,
        scratch=(long, pltpu.VMEM((rows, SUB, LANES), f32)),
        name="taps",
        flops=macs,
    )
    block, later = lax.optimization_barrier((block, later))
    near = lax.axis_size(NEAR)
    block = block.reshape(near, rows // near, width + LANES)
    block = lax.all_to_all(block, NEAR, 0, 0)
    block = jnp.sum(block.astype(f32), 0).astype(bf16)
    block, grad_conv, later = lax.optimization_barrier((block, grad_conv, later))
    block = shared(block, FAR)
    grad_k, grad_v = call(
        back_kernel,
        (struct((rows, width), bf16), struct((rows, width), bf16)),
        grad_conv,
        later,
        filters,
        k_proj,
        v_proj,
        scratch=(long,),
        name="back",
        flops=macs,
    )
    block = jnp.sum(block.astype(f32), 0).astype(bf16)
    block, grad_k = lax.optimization_barrier((block, grad_k))
    whole = shared(block, NEAR).reshape(rows, width + LANES)
    grad_filters, grad_gain = call(
        final_kernel,
        (struct((rows, width), f32), struct((width // LANES, LANES), f32)),
        whole,
        name="final",
        flops=0,
    )
    return (grad_q, grad_k, grad_v, grad_filters, grad_gain.reshape(width))


def solution(mesh):
    cube = 4
    far = mesh.devices.shape[0] // (cube * cube)
    split = Mesh(mesh.devices.reshape(far, cube, cube, -1), (*CTX, "tp"))
    rows = P(CTX, "tp")
    in_specs = (rows, rows, rows, rows, P(None, "tp"), P("tp"))
    out_specs = (rows, rows, rows, P(None, "tp"), P("tp"))
    return jax.shard_map(shards, mesh=split, in_specs=in_specs, out_specs=out_specs, check_vma=False)
```

```python
import jax
import jax.numpy as jnp
from jax import lax
from jax.experimental import pallas as pl
from jax.experimental.pallas import tpu as pltpu
from jax.sharding import Mesh, PartitionSpec as P

D = 8192
CTX = ("zh", "zl", "x")
NEAR = ("zl", "x")
FAR = "zh"
OUTWARDS = (((0, 1),), ((0, 4), (1, 2)), ((0, 7), (2, 3), (4, 5)), ((7, 6),))
LANES = 128
SUB = 8
VMEM_BYTES = 8 << 20


epsilon = 1e-06
f32 = jnp.float32
bf16 = jnp.bfloat16


def passed_along(value, by):
    length = lax.axis_size(CTX)
    pairs = [(i, i + by) for i in range(length) if 0 <= i + by < length]
    return lax.ppermute(value, CTX, pairs)


def shared(value, axes):
    size = lax.axis_size(axes)
    copies = jnp.broadcast_to(value[None], (size, *value.shape))
    return lax.all_to_all(copies, axes, 0, 0)


def far_sum(value):
    cubes = lax.axis_size(FAR)
    assert cubes == 8
    parts = [lax.ppermute(value, FAR, [(i, 0)]) for i in range(1, cubes)]

    def total(extra):
        (*given, _) = lax.optimization_barrier((value, *parts, extra))
        whole = sum(part.astype(f32) for part in given).astype(bf16)
        whole = jnp.where(lax.axis_index(FAR) == 0, whole, jnp.zeros_like(whole))
        for pairs in OUTWARDS:
            whole = whole + lax.ppermute(whole, FAR, pairs)
        return whole

    return total


def call(kernel, outs, *operands, scratch=(), name, flops):
    in_vmem = pl.BlockSpec(memory_space=pltpu.VMEM)
    moved = sum(x.size * x.dtype.itemsize for x in (*operands, *outs))
    return pl.pallas_call(
        kernel,
        out_shape=outs,
        in_specs=[in_vmem] * len(operands),
        out_specs=tuple(in_vmem for _ in outs),
        scratch_shapes=list(scratch),
        name=name,
        compiler_params=pltpu.CompilerParams(vmem_limit_bytes=VMEM_BYTES),
        cost_estimate=pl.CostEstimate(flops=flops, bytes_accessed=moved, transcendentals=0),
    )(*operands)


def struct(shape, dtype):
    return jax.ShapeDtypeStruct(shape, dtype)


def over_tiles(width, body):
    def step(tile, carry):
        body(tile, pl.ds(pl.multiple_of(tile * LANES, LANES), LANES))
        return carry

    lax.fori_loop(0, width // LANES, step, 0)


def blocks(value):
    return [value[SUB * i : SUB * i + SUB] for i in range(value.shape[0] // SUB)]


def fill(window, at, value):
    window[pl.ds(at, value.shape[0]), :] = value.astype(f32)


def own_kernel(mixed, filters, conv, window):
    rows, width = mixed.shape
    count = rows // SUB
    window[pl.ds(0, SUB), :] = jnp.zeros((SUB, LANES), f32)

    def tile(_, lanes):
        fill(window, SUB, mixed[:, lanes])
        total = [None] * count
        for shift in range(SUB):
            slid = [window[pl.ds(SUB + SUB * i - shift, SUB), :] for i in range(count)]
            for step in range(count):
                weight = filters[pl.ds(SUB * step + shift, 1), lanes]
                for i in range(step, count):
                    term = weight * slid[i - step]
                    total[i] = term if total[i] is None else total[i] + term
        for i in range(count):
            conv[pl.ds(SUB * i, SUB), lanes] = total[i]

    over_tiles(width, tile)


def rim_kernel(own, earlier, filters, query, cot, gain, conv, sums, window, squares, crosses):
    rows, width = own.shape
    count = rows // SUB
    window[pl.ds(rows, SUB), :] = jnp.zeros((SUB, LANES), f32)
    squares[...] = jnp.zeros(squares.shape, f32)
    crosses[...] = jnp.zeros(crosses.shape, f32)

    def tile(_, lanes):
        fill(window, 0, earlier[:, lanes])
        total = [own[pl.ds(SUB * i, SUB), lanes] for i in range(count)]
        for shift in range(SUB):
            slid = [window[pl.ds(rows - SUB * i - shift, SUB), :] for i in range(count)]
            for step in range(count):
                weight = filters[pl.ds(SUB * step + shift, 1), lanes]
                for i in range(step + 1):
                    total[i] = total[i] + weight * slid[step - i]
        for i in range(count):
            at = pl.ds(SUB * i, SUB)
            conv[at, lanes] = total[i]
        whole = conv[:, lanes]
        product = query[:, lanes].astype(f32) * whole
        weighted = gain[:, lanes] * cot[:, lanes].astype(f32)
        squares[...] += product * product
        crosses[...] += weighted * product

    over_tiles(width, tile)
    square = jnp.sum(squares[...].T, 0, keepdims=True)
    cross = jnp.sum(crosses[...].T, 0, keepdims=True)
    first = lax.broadcasted_iota(jnp.int32, sums.shape[1:], 0) == 0
    both = jnp.where(first, square, cross)
    for i in range(sums.shape[0]):
        sums[i] = both


def gathered(parts):
    row = lax.broadcasted_iota(jnp.int32, (SUB, LANES), 0)
    half = 1
    while half < SUB:
        low = (row & half) == 0
        parts = [
            jnp.where(low, a, b) + pltpu.roll(jnp.where(low, b, a), half, 0)
            for a, b in zip(parts[::2], parts[1::2])
        ]
        half *= 2
    return parts[0]


def grads_kernel(
    sums, conv, query, cot, gain, earlier, mixed, grad_conv, grad_q, block, window, inverse, pull, partial
):
    rows, width = conv.shape
    count = rows // SUB
    both = jnp.sum(sums[...], 0)
    rms = jnp.sqrt(both[0:1] / D + epsilon)
    inverse[...] = jnp.broadcast_to(1.0 / rms, (LANES, rows)).T
    pull[...] = jnp.broadcast_to(both[1:2] / (D * (rms * rms * rms)), (LANES, rows)).T
    block[:, width:] = jnp.zeros((rows, LANES), bf16)

    def tile(index, lanes):
        whole = conv[:, lanes]
        query_f32 = query[:, lanes].astype(f32)
        cot_f32 = cot[:, lanes].astype(f32)
        product = query_f32 * whole
        grad_product = gain[:, lanes] * cot_f32 * inverse[...] - product * pull[...]
        rounded = (query_f32 * grad_product).astype(bf16)
        grad_conv[:, lanes] = rounded
        grad_q[:, lanes] = (grad_product * whole).astype(bf16)
        gains = jnp.sum((cot_f32 * product * inverse[...]).reshape(count, SUB, LANES), 0)
        block[pl.ds(pl.multiple_of(index * SUB, SUB), SUB), width:] = gains.astype(bf16)
        fill(window, 0, earlier[:, lanes])
        fill(window, rows, mixed[:, lanes])
        ours = blocks(rounded.astype(f32))
        for shift in range(SUB):
            slid = [window[pl.ds(SUB * (i + 1) - shift, SUB), :] for i in range(2 * count - 1)]
            for step in range(count):
                terms = [ours[i] * slid[count - 1 + i - step] for i in range(count)]
                while len(terms) > 1:
                    terms = [a + b for a, b in zip(terms[::2], terms[1::2])]
                partial[SUB * step + shift] = terms[0]
        for step in range(0, count, 2):
            pair = [gathered([partial[SUB * s + i] for i in range(SUB)]) for s in (step, step + 1)]
            block[pl.ds(SUB * step, 2 * SUB), lanes] = jnp.concatenate(pair, 0).astype(bf16)

    over_tiles(width, tile)


def back_kernel(grad_conv, later, filters, k_proj, v_proj, grad_k, grad_v, window):
    rows, width = grad_conv.shape
    count = rows // SUB

    def tile(_, lanes):
        fill(window, 0, grad_conv[:, lanes])
        fill(window, rows, later[:, lanes])
        total = [jnp.zeros((SUB, LANES), f32)] * count
        for shift in range(SUB):
            slid = [window[pl.ds(SUB * i + shift, SUB), :] for i in range(2 * count - 1)]
            for step in range(count):
                weight = filters[pl.ds(SUB * step + shift, 1), lanes]
                for i in range(count):
                    total[i] = total[i] + weight * slid[i + step]
        grad_mixed = jnp.concatenate(total, 0)
        grad_k[:, lanes] = (grad_mixed * v_proj[:, lanes].astype(f32)).astype(bf16)
        grad_v[:, lanes] = (grad_mixed * k_proj[:, lanes].astype(f32)).astype(bf16)

    over_tiles(width, tile)


def final_kernel(whole, grad_filters, grad_gain):
    width = grad_filters.shape[1]
    grad_filters[...] = whole[:, :width].astype(f32)
    for i in range(width // LANES):
        part = whole[pl.ds(SUB * i, SUB), width:].astype(f32)
        grad_gain[pl.ds(i, 1), :] = jnp.sum(part, 0, keepdims=True)


def shards(q_proj, k_proj, v_proj, cotangent, filters, gain):
    rows, width = q_proj.shape
    macs = 2 * filters.shape[0] * rows * width
    tile = pltpu.VMEM((rows, LANES), f32)
    short = pltpu.VMEM((rows + SUB, LANES), f32)
    long = pltpu.VMEM((2 * rows, LANES), f32)
    gain = gain.reshape(1, width)
    mixed = (k_proj.astype(f32) * v_proj.astype(f32)).astype(bf16)
    earlier = passed_along(mixed, 1)
    (own,) = call(
        own_kernel, (struct((rows, width), f32),), mixed, filters, scratch=(short,), name="own", flops=macs // 2
    )
    members = lax.axis_size("tp")
    conv, sums = call(
        rim_kernel,
        (struct((rows, width), f32), struct((members, SUB, rows), f32)),
        own,
        earlier,
        filters,
        q_proj,
        cotangent,
        gain,
        scratch=(short, tile, tile),
        name="rim",
        flops=macs // 2,
    )
    sums = lax.all_to_all(sums, "tp", 0, 0)
    grad_conv, grad_q, block = call(
        grads_kernel,
        (struct((rows, width), bf16), struct((rows, width), bf16), struct((rows, width + LANES), bf16)),
        sums,
        conv,
        q_proj,
        cotangent,
        gain,
        earlier,
        mixed,
        scratch=(long, tile, tile, pltpu.VMEM((rows, SUB, LANES), f32)),
        name="grads",
        flops=macs,
    )
    near = lax.axis_size(NEAR)
    block = block.reshape(near, rows // near, width + LANES)
    block = lax.all_to_all(block, NEAR, 0, 0)
    block = jnp.sum(block.astype(f32), 0).astype(bf16)
    block, grad_conv = lax.optimization_barrier((block, grad_conv))
    total = far_sum(block)
    later = passed_along(grad_conv, -1)
    grad_k, grad_v = call(
        back_kernel,
        (struct((rows, width), bf16), struct((rows, width), bf16)),
        grad_conv,
        later,
        filters,
        k_proj,
        v_proj,
        scratch=(long,),
        name="back",
        flops=macs,
    )
    whole = shared(total(grad_k), NEAR).reshape(rows, width + LANES)
    grad_filters, grad_gain = call(
        final_kernel,
        (struct((rows, width), f32), struct((width // LANES, LANES), f32)),
        whole,
        name="final",
        flops=0,
    )
    return (grad_q, grad_k, grad_v, grad_filters, grad_gain.reshape(width))


def solution(mesh):
    cube = 4
    far = mesh.devices.shape[0] // (cube * cube)
    split = Mesh(mesh.devices.reshape(far, cube, cube, -1), (*CTX, "tp"))
    rows = P(CTX, "tp")
    in_specs = (rows, rows, rows, rows, P(None, "tp"), P("tp"))
    out_specs = (rows, rows, rows, P(None, "tp"), P("tp"))
    return jax.shard_map(shards, mesh=split, in_specs=in_specs, out_specs=out_specs, check_vma=False)
```

```python
import jax
import jax.numpy as jnp
from jax import lax
from jax.experimental import pallas as pl
from jax.experimental.pallas import tpu as pltpu
from jax.sharding import Mesh, PartitionSpec as P

D = 8192
CTX = ("zh", "zl", "x")
NEAR = ("zl", "x")
FAR = "zh"
INWARDS = (4, 3, 5, 2, 6, 1, 7)
OUTWARDS = ((((0, 1),), ((0, 7),)), (((7, 4), (1, 2)),), (((7, 6), (2, 3), (4, 5)),))
LANES = 128
SUB = 8
VMEM_BYTES = 8 << 20


epsilon = 1e-06
f32 = jnp.float32
bf16 = jnp.bfloat16


def passed_along(value, by):
    length = lax.axis_size(CTX)
    pairs = [(i, i + by) for i in range(length) if 0 <= i + by < length]
    return lax.ppermute(value, CTX, pairs)


def shared(value, axes):
    size = lax.axis_size(axes)
    copies = jnp.broadcast_to(value[None], (size, *value.shape))
    return lax.all_to_all(copies, axes, 0, 0)


def far_sum(value):
    assert lax.axis_size(FAR) == 1 + len(INWARDS)
    parts = []
    for cube in INWARDS:
        parts.append(lax.ppermute(value, FAR, [(cube, 0)]))

    def total(extra):
        (*given, _) = lax.optimization_barrier((value, *parts, extra))
        whole = sum(part.astype(f32) for part in given).astype(bf16)
        whole = jnp.where(lax.axis_index(FAR) == 0, whole, jnp.zeros_like(whole))
        for steps in OUTWARDS:
            whole = sum([lax.ppermute(whole, FAR, pairs) for pairs in steps], whole)
        return whole

    return total


def call(kernel, outs, *operands, scratch=(), flops):
    in_vmem = pl.BlockSpec(memory_space=pltpu.VMEM)
    moved = sum(x.size * x.dtype.itemsize for x in (*operands, *outs))
    return pl.pallas_call(
        kernel,
        out_shape=outs,
        in_specs=[in_vmem] * len(operands),
        out_specs=tuple(in_vmem for _ in outs),
        scratch_shapes=list(scratch),
        compiler_params=pltpu.CompilerParams(vmem_limit_bytes=VMEM_BYTES),
        cost_estimate=pl.CostEstimate(flops=flops, bytes_accessed=moved, transcendentals=0),
    )(*operands)


def struct(shape, dtype):
    return jax.ShapeDtypeStruct(shape, dtype)


def over_tiles(width, body):
    def step(tile, carry):
        body(tile, pl.ds(pl.multiple_of(tile * LANES, LANES), LANES))
        return carry

    lax.fori_loop(0, width // LANES, step, 0)


def blocks(value):
    return [value[SUB * i : SUB * i + SUB] for i in range(value.shape[0] // SUB)]


def fill(window, at, value):
    window[pl.ds(at, value.shape[0]), :] = value.astype(f32)


def own_kernel(mixed, filters, conv, window):
    rows, width = mixed.shape
    count = rows // SUB
    window[pl.ds(0, SUB), :] = jnp.zeros((SUB, LANES), f32)

    def tile(_, lanes):
        fill(window, SUB, mixed[:, lanes])
        total = [None] * count
        for shift in range(SUB):
            slid = [window[pl.ds(SUB + SUB * i - shift, SUB), :] for i in range(count)]
            for step in range(count):
                weight = filters[pl.ds(SUB * step + shift, 1), lanes]
                for i in range(step, count):
                    term = weight * slid[i - step]
                    total[i] = term if total[i] is None else total[i] + term
        for i in range(count):
            conv[pl.ds(SUB * i, SUB), lanes] = total[i]

    over_tiles(width, tile)


def rim_kernel(own, earlier, filters, query, cot, gain, conv, sums, window, squares, crosses):
    rows, width = own.shape
    count = rows // SUB
    window[pl.ds(rows, SUB), :] = jnp.zeros((SUB, LANES), f32)
    squares[...] = jnp.zeros(squares.shape, f32)
    crosses[...] = jnp.zeros(crosses.shape, f32)

    def tile(_, lanes):
        fill(window, 0, earlier[:, lanes])
        total = [own[pl.ds(SUB * i, SUB), lanes] for i in range(count)]
        for shift in range(SUB):
            slid = [window[pl.ds(rows - SUB * i - shift, SUB), :] for i in range(count)]
            for step in range(count):
                weight = filters[pl.ds(SUB * step + shift, 1), lanes]
                for i in range(step + 1):
                    total[i] = total[i] + weight * slid[step - i]
        for i in range(count):
            at = pl.ds(SUB * i, SUB)
            conv[at, lanes] = total[i]
        whole = conv[:, lanes]
        product = query[:, lanes].astype(f32) * whole
        weighted = gain[:, lanes] * cot[:, lanes].astype(f32)
        squares[...] += product * product
        crosses[...] += weighted * product

    over_tiles(width, tile)
    square = jnp.sum(squares[...].T, 0, keepdims=True)
    cross = jnp.sum(crosses[...].T, 0, keepdims=True)
    first = lax.broadcasted_iota(jnp.int32, sums.shape[1:], 0) == 0
    both = jnp.where(first, square, cross)
    for i in range(sums.shape[0]):
        sums[i] = both


def gathered(parts):
    row = lax.broadcasted_iota(jnp.int32, (SUB, LANES), 0)
    half = 1
    while half < SUB:
        low = (row & half) == 0
        parts = [
            jnp.where(low, a, b) + pltpu.roll(jnp.where(low, b, a), half, 0)
            for a, b in zip(parts[::2], parts[1::2])
        ]
        half *= 2
    return parts[0]


def grads_kernel(
    sums, conv, query, cot, gain, earlier, mixed, grad_conv, grad_q, block, window, inverse, pull, partial
):
    rows, width = conv.shape
    count = rows // SUB
    both = jnp.sum(sums[...], 0)
    rms = jnp.sqrt(both[0:1] / D + epsilon)
    inverse[...] = jnp.broadcast_to(1.0 / rms, (LANES, rows)).T
    pull[...] = jnp.broadcast_to(both[1:2] / (D * (rms * rms * rms)), (LANES, rows)).T
    block[:, width:] = jnp.zeros((rows, LANES), bf16)

    def tile(index, lanes):
        whole = conv[:, lanes]
        query_f32 = query[:, lanes].astype(f32)
        cot_f32 = cot[:, lanes].astype(f32)
        product = query_f32 * whole
        grad_product = gain[:, lanes] * cot_f32 * inverse[...] - product * pull[...]
        rounded = (query_f32 * grad_product).astype(bf16)
        grad_conv[:, lanes] = rounded
        grad_q[:, lanes] = (grad_product * whole).astype(bf16)
        gains = jnp.sum((cot_f32 * product * inverse[...]).reshape(count, SUB, LANES), 0)
        block[pl.ds(pl.multiple_of(index * SUB, SUB), SUB), width:] = gains.astype(bf16)
        fill(window, 0, earlier[:, lanes])
        fill(window, rows, mixed[:, lanes])
        ours = blocks(rounded.astype(f32))
        for shift in range(SUB):
            slid = [window[pl.ds(SUB * (i + 1) - shift, SUB), :] for i in range(2 * count - 1)]
            for step in range(count):
                terms = [ours[i] * slid[count - 1 + i - step] for i in range(count)]
                while len(terms) > 1:
                    terms = [a + b for a, b in zip(terms[::2], terms[1::2])]
                partial[SUB * step + shift] = terms[0]
        for step in range(0, count, 2):
            pair = [gathered([partial[SUB * s + i] for i in range(SUB)]) for s in (step, step + 1)]
            block[pl.ds(SUB * step, 2 * SUB), lanes] = jnp.concatenate(pair, 0).astype(bf16)

    over_tiles(width, tile)


def back_kernel(grad_conv, later, filters, k_proj, v_proj, grad_k, grad_v, window):
    rows, width = grad_conv.shape
    count = rows // SUB

    def tile(_, lanes):
        fill(window, 0, grad_conv[:, lanes])
        fill(window, rows, later[:, lanes])
        total = [jnp.zeros((SUB, LANES), f32)] * count
        for shift in range(SUB):
            slid = [window[pl.ds(SUB * i + shift, SUB), :] for i in range(2 * count - 1)]
            for step in range(count):
                weight = filters[pl.ds(SUB * step + shift, 1), lanes]
                for i in range(count):
                    total[i] = total[i] + weight * slid[i + step]
        grad_mixed = jnp.concatenate(total, 0)
        grad_k[:, lanes] = (grad_mixed * v_proj[:, lanes].astype(f32)).astype(bf16)
        grad_v[:, lanes] = (grad_mixed * k_proj[:, lanes].astype(f32)).astype(bf16)

    over_tiles(width, tile)


def final_kernel(whole, grad_filters, grad_gain):
    width = grad_filters.shape[1]
    grad_filters[...] = whole[:, :width].astype(f32)
    for i in range(width // LANES):
        part = whole[pl.ds(SUB * i, SUB), width:].astype(f32)
        grad_gain[pl.ds(i, 1), :] = jnp.sum(part, 0, keepdims=True)


def device_part(q_proj, k_proj, v_proj, cotangent, filters, gain):
    rows, width = q_proj.shape
    macs = 2 * filters.shape[0] * rows * width
    tile = pltpu.VMEM((rows, LANES), f32)
    short = pltpu.VMEM((rows + SUB, LANES), f32)
    long = pltpu.VMEM((2 * rows, LANES), f32)
    gain = gain.reshape(1, width)
    mixed = (k_proj.astype(f32) * v_proj.astype(f32)).astype(bf16)
    earlier = passed_along(mixed, 1)
    (own,) = call(
        own_kernel, (struct((rows, width), f32),), mixed, filters, scratch=(short,), flops=macs // 2
    )
    members = lax.axis_size("tp")
    conv, sums = call(
        rim_kernel,
        (struct((rows, width), f32), struct((members, SUB, rows), f32)),
        own,
        earlier,
        filters,
        q_proj,
        cotangent,
        gain,
        scratch=(short, tile, tile),
        flops=macs // 2,
    )
    sums = lax.all_to_all(sums, "tp", 0, 0)
    grad_conv, grad_q, block = call(
        grads_kernel,
        (struct((rows, width), bf16), struct((rows, width), bf16), struct((rows, width + LANES), bf16)),
        sums,
        conv,
        q_proj,
        cotangent,
        gain,
        earlier,
        mixed,
        scratch=(long, tile, tile, pltpu.VMEM((rows, SUB, LANES), f32)),
        flops=macs,
    )
    near = lax.axis_size(NEAR)
    block = block.reshape(near, rows // near, width + LANES)
    block = lax.all_to_all(block, NEAR, 0, 0)
    block = jnp.sum(block.astype(f32), 0).astype(bf16)
    block, grad_conv = lax.optimization_barrier((block, grad_conv))
    total = far_sum(block)
    later = passed_along(grad_conv, -1)
    grad_k, grad_v = call(
        back_kernel,
        (struct((rows, width), bf16), struct((rows, width), bf16)),
        grad_conv,
        later,
        filters,
        k_proj,
        v_proj,
        scratch=(long,),
        flops=macs,
    )
    whole = shared(total(grad_k), NEAR).reshape(rows, width + LANES)
    grad_filters, grad_gain = call(
        final_kernel,
        (struct((rows, width), f32), struct((width // LANES, LANES), f32)),
        whole,
        flops=0,
    )
    return (grad_q, grad_k, grad_v, grad_filters, grad_gain.reshape(width))


def solution(mesh):
    cube = 4
    far = mesh.devices.shape[0] // (cube * cube)
    split = Mesh(mesh.devices.reshape(far, cube, cube, -1), (*CTX, "tp"))
    rows = P(CTX, "tp")
    in_specs = (rows, rows, rows, rows, P(None, "tp"), P("tp"))
    out_specs = (rows, rows, rows, P(None, "tp"), P("tp"))
    return jax.shard_map(device_part, mesh=split, in_specs=in_specs, out_specs=out_specs, check_vma=False)
```

```python
import jax
import jax.numpy as jnp
from jax import lax
from jax.experimental import pallas as pl
from jax.experimental.pallas import tpu as pltpu
from jax.sharding import Mesh, PartitionSpec as P

D = 8192
CTX = ("zh", "zl", "x")
NEAR = ("zl", "x")
FAR = "zh"
INWARDS = (4, 3, 5, 2, 6, 1, 7)
OUTWARDS = ((((0, 1),), ((0, 7),)), (((7, 5), (1, 2)),), (((7, 6), (2, 3), (5, 4)),))
EARLY = 1
LANES = 128
SUB = 8
VMEM_BYTES = 8 << 20


epsilon = 1e-06
f32 = jnp.float32
bf16 = jnp.bfloat16


def passed_along(value, by):
    length = lax.axis_size(CTX)
    pairs = [(i, i + by) for i in range(length) if 0 <= i + by < length]
    return lax.ppermute(value, CTX, pairs)


def shared(value, axes):
    size = lax.axis_size(axes)
    copies = jnp.broadcast_to(value[None], (size, *value.shape))
    return lax.all_to_all(copies, axes, 0, 0)


def far_sum(value):
    assert lax.axis_size(FAR) == 1 + len(INWARDS)
    parts = []
    for cube in INWARDS:
        parts.append(lax.ppermute(value, FAR, [(cube, 0)]))

    def total(extra):
        (*given, _) = lax.optimization_barrier((value, *parts, extra))
        whole = sum(part.astype(f32) for part in given).astype(bf16)
        whole = jnp.where(lax.axis_index(FAR) == 0, whole, jnp.zeros_like(whole))
        for steps in OUTWARDS:
            moved = []
            for pairs in steps:
                moved.append(lax.ppermute(whole, FAR, pairs))
            whole = sum(moved, whole)
        return whole

    return total


def call(kernel, outs, *operands, scratch=(), flops):
    in_vmem = pl.BlockSpec(memory_space=pltpu.VMEM)
    in_smem = pl.BlockSpec(memory_space=pltpu.SMEM)
    moved = sum(x.size * x.dtype.itemsize for x in (*operands, *outs))
    return pl.pallas_call(
        kernel,
        out_shape=outs,
        in_specs=[in_smem if x.dtype == jnp.int32 else in_vmem for x in operands],
        out_specs=tuple(in_vmem for _ in outs),
        scratch_shapes=list(scratch),
        compiler_params=pltpu.CompilerParams(vmem_limit_bytes=VMEM_BYTES),
        cost_estimate=pl.CostEstimate(flops=flops, bytes_accessed=moved, transcendentals=0),
    )(*operands)


def struct(shape, dtype):
    return jax.ShapeDtypeStruct(shape, dtype)


def over_tiles(width, body):
    def step(tile, carry):
        body(tile, pl.ds(pl.multiple_of(tile * LANES, LANES), LANES))
        return carry

    lax.fori_loop(0, width // LANES, step, 0)


def blocks(value):
    return [value[SUB * i : SUB * i + SUB] for i in range(value.shape[0] // SUB)]


def fill(window, at, value):
    window[pl.ds(at, value.shape[0]), :] = value.astype(f32)


def own_kernel(mixed, filters, conv, window):
    rows, width = mixed.shape
    count = rows // SUB
    window[pl.ds(0, SUB), :] = jnp.zeros((SUB, LANES), f32)

    def tile(_, lanes):
        fill(window, SUB, mixed[:, lanes])
        total = [None] * count
        for shift in range(SUB):
            slid = [window[pl.ds(SUB + SUB * i - shift, SUB), :] for i in range(count)]
            for step in range(count):
                weight = filters[pl.ds(SUB * step + shift, 1), lanes]
                for i in range(step, count):
                    term = weight * slid[i - step]
                    total[i] = term if total[i] is None else total[i] + term
        for i in range(count):
            conv[pl.ds(SUB * i, SUB), lanes] = total[i]

    over_tiles(width, tile)


def rim_kernel(own, earlier, filters, query, cot, gain, conv, sums, window, squares, crosses):
    rows, width = own.shape
    count = rows // SUB
    window[pl.ds(rows, SUB), :] = jnp.zeros((SUB, LANES), f32)
    squares[...] = jnp.zeros(squares.shape, f32)
    crosses[...] = jnp.zeros(crosses.shape, f32)

    def tile(_, lanes):
        fill(window, 0, earlier[:, lanes])
        total = [own[pl.ds(SUB * i, SUB), lanes] for i in range(count)]
        for shift in range(SUB):
            slid = [window[pl.ds(rows - SUB * i - shift, SUB), :] for i in range(count)]
            for step in range(count):
                weight = filters[pl.ds(SUB * step + shift, 1), lanes]
                for i in range(step + 1):
                    total[i] = total[i] + weight * slid[step - i]
        for i in range(count):
            at = pl.ds(SUB * i, SUB)
            conv[at, lanes] = total[i]
        whole = conv[:, lanes]
        product = query[:, lanes].astype(f32) * whole
        weighted = gain[:, lanes] * cot[:, lanes].astype(f32)
        squares[...] += product * product
        crosses[...] += weighted * product

    over_tiles(width, tile)
    square = jnp.sum(squares[...].T, 0, keepdims=True)
    cross = jnp.sum(crosses[...].T, 0, keepdims=True)
    first = lax.broadcasted_iota(jnp.int32, sums.shape[1:], 0) == 0
    both = jnp.where(first, square, cross)
    for i in range(sums.shape[0]):
        sums[i] = both


def gathered(parts):
    row = lax.broadcasted_iota(jnp.int32, (SUB, LANES), 0)
    half = 1
    while half < SUB:
        low = (row & half) == 0
        parts = [
            jnp.where(low, a, b) + pltpu.roll(jnp.where(low, b, a), half, 0)
            for a, b in zip(parts[::2], parts[1::2])
        ]
        half *= 2
    return parts[0]


def grads_kernel(
    sums, conv, query, cot, gain, earlier, mixed, grad_conv, grad_q, block, window, inverse, pull, partial
):
    rows, width = conv.shape
    count = rows // SUB
    both = jnp.sum(sums[...], 0)
    rms = jnp.sqrt(both[0:1] / D + epsilon)
    inverse[...] = jnp.broadcast_to(1.0 / rms, (LANES, rows)).T
    pull[...] = jnp.broadcast_to(both[1:2] / (D * (rms * rms * rms)), (LANES, rows)).T
    block[:, width:] = jnp.zeros((rows, LANES), bf16)

    def tile(index, lanes):
        whole = conv[:, lanes]
        query_f32 = query[:, lanes].astype(f32)
        cot_f32 = cot[:, lanes].astype(f32)
        product = query_f32 * whole
        grad_product = gain[:, lanes] * cot_f32 * inverse[...] - product * pull[...]
        rounded = (query_f32 * grad_product).astype(bf16)
        grad_conv[:, lanes] = rounded
        grad_q[:, lanes] = (grad_product * whole).astype(bf16)
        gains = jnp.sum((cot_f32 * product * inverse[...]).reshape(count, SUB, LANES), 0)
        block[pl.ds(pl.multiple_of(index * SUB, SUB), SUB), width:] = gains.astype(bf16)
        fill(window, 0, earlier[:, lanes])
        fill(window, rows, mixed[:, lanes])
        ours = blocks(rounded.astype(f32))
        for shift in range(SUB):
            slid = [window[pl.ds(SUB * (i + 1) - shift, SUB), :] for i in range(2 * count - 1)]
            for step in range(count):
                terms = [ours[i] * slid[count - 1 + i - step] for i in range(count)]
                while len(terms) > 1:
                    terms = [a + b for a, b in zip(terms[::2], terms[1::2])]
                partial[SUB * step + shift] = terms[0]
        for step in range(0, count, 2):
            pair = [gathered([partial[SUB * s + i] for i in range(SUB)]) for s in (step, step + 1)]
            block[pl.ds(SUB * step, 2 * SUB), lanes] = jnp.concatenate(pair, 0).astype(bf16)

    over_tiles(width, tile)


def back(grad_conv, later, filters, k_proj, v_proj, grad_k, grad_v, window):
    rows, width = grad_conv.shape
    count = rows // SUB

    def tile(_, lanes):
        fill(window, 0, grad_conv[:, lanes])
        fill(window, rows, later[:, lanes])
        total = [jnp.zeros((SUB, LANES), f32)] * count
        for shift in range(SUB):
            slid = [window[pl.ds(SUB * i + shift, SUB), :] for i in range(2 * count - 1)]
            for step in range(count):
                weight = filters[pl.ds(SUB * step + shift, 1), lanes]
                for i in range(count):
                    total[i] = total[i] + weight * slid[i + step]
        grad_mixed = jnp.concatenate(total, 0)
        grad_k[:, lanes] = (grad_mixed * v_proj[:, lanes].astype(f32)).astype(bf16)
        grad_v[:, lanes] = (grad_mixed * k_proj[:, lanes].astype(f32)).astype(bf16)

    over_tiles(width, tile)


def early_back_kernel(early, *refs):
    @pl.when(early[0] == 1)
    def _():
        back(*refs)


def late_back_kernel(early, early_k, early_v, *refs):
    grad_k, grad_v = refs[-3:-1]

    @pl.when(early[0] == 1)
    def _():
        grad_k[...] = early_k[...]
        grad_v[...] = early_v[...]

    @pl.when(early[0] == 0)
    def _():
        back(*refs)


def final_kernel(whole, grad_filters, grad_gain):
    width = grad_filters.shape[1]
    grad_filters[...] = whole[:, :width].astype(f32)
    for i in range(width // LANES):
        part = whole[pl.ds(SUB * i, SUB), width:].astype(f32)
        grad_gain[pl.ds(i, 1), :] = jnp.sum(part, 0, keepdims=True)


def device_part(q_proj, k_proj, v_proj, cotangent, filters, gain):
    rows, width = q_proj.shape
    macs = 2 * filters.shape[0] * rows * width
    tile = pltpu.VMEM((rows, LANES), f32)
    short = pltpu.VMEM((rows + SUB, LANES), f32)
    long = pltpu.VMEM((2 * rows, LANES), f32)
    gain = gain.reshape(1, width)
    mixed = (k_proj.astype(f32) * v_proj.astype(f32)).astype(bf16)
    earlier = passed_along(mixed, 1)
    (own,) = call(own_kernel, (struct((rows, width), f32),), mixed, filters, scratch=(short,), flops=macs // 2)
    members = lax.axis_size("tp")
    conv, sums = call(
        rim_kernel,
        (struct((rows, width), f32), struct((members, SUB, rows), f32)),
        own,
        earlier,
        filters,
        q_proj,
        cotangent,
        gain,
        scratch=(short, tile, tile),
        flops=macs // 2,
    )
    sums = lax.all_to_all(sums, "tp", 0, 0)
    grad_conv, grad_q, block = call(
        grads_kernel,
        (struct((rows, width), bf16), struct((rows, width), bf16), struct((rows, width + LANES), bf16)),
        sums,
        conv,
        q_proj,
        cotangent,
        gain,
        earlier,
        mixed,
        scratch=(long, tile, tile, pltpu.VMEM((rows, SUB, LANES), f32)),
        flops=macs,
    )
    near = lax.axis_size(NEAR)
    block = block.reshape(near, rows // near, width + LANES)
    block = lax.all_to_all(block, NEAR, 0, 0)
    block = jnp.sum(block.astype(f32), 0).astype(bf16)
    block, grad_conv = lax.optimization_barrier((block, grad_conv))
    total = far_sum(block)
    later = passed_along(grad_conv, -1)
    early = (lax.axis_index(FAR) < EARLY).astype(jnp.int32).reshape(1)
    grads = (struct((rows, width), bf16), struct((rows, width), bf16))
    sources = (grad_conv, later, filters, k_proj, v_proj)
    early_k, early_v = call(early_back_kernel, grads, early, *sources, scratch=(long,), flops=macs)
    whole = total(early_k)
    grad_k, grad_v = call(late_back_kernel, grads, early, early_k, early_v, *sources, scratch=(long,), flops=macs)
    whole, grad_k = lax.optimization_barrier((whole, grad_k))
    whole = shared(whole, NEAR).reshape(rows, width + LANES)
    grad_filters, grad_gain = call(
        final_kernel, (struct((rows, width), f32), struct((width // LANES, LANES), f32)), whole, flops=0
    )
    return (grad_q, grad_k, grad_v, grad_filters, grad_gain.reshape(width))


def solution(mesh):
    cube = 4
    far = mesh.devices.shape[0] // (cube * cube)
    split = Mesh(mesh.devices.reshape(far, cube, cube, -1), (*CTX, "tp"))
    rows = P(CTX, "tp")
    in_specs = (rows, rows, rows, rows, P(None, "tp"), P("tp"))
    out_specs = (rows, rows, rows, P(None, "tp"), P("tp"))
    return jax.shard_map(device_part, mesh=split, in_specs=in_specs, out_specs=out_specs, check_vma=False)
```

```python
import jax
import jax.numpy as jnp
from jax import lax
from jax.experimental import pallas as pl
from jax.experimental.pallas import tpu as pltpu
from jax.sharding import Mesh, PartitionSpec as P

D = 8192
CTX = ("zh", "zl", "x")
NEAR = ("zl", "x")
FAR = "zh"
INWARDS = (4, 5, 3, 2, 6, 1, 7)
OUTWARDS = (
    (((0, 1),), ((0, 7),)),
    (((7, 4), (1, 2)), ((7, 5),)),
    (((7, 6), (2, 3)),),
)
EARLY = 1
LANES = 128
SUB = 8
VMEM_BYTES = 8 << 20


epsilon = 1e-06
f32 = jnp.float32
bf16 = jnp.bfloat16


def passed_along(value, by):
    length = lax.axis_size(CTX)
    pairs = [(i, i + by) for i in range(length) if 0 <= i + by < length]
    return lax.ppermute(value, CTX, pairs)


def shared(value, axes):
    size = lax.axis_size(axes)
    copies = jnp.broadcast_to(value[None], (size, *value.shape))
    return lax.all_to_all(copies, axes, 0, 0)


def far_sum(value):
    assert lax.axis_size(FAR) == 1 + len(INWARDS)
    parts = []
    for cube in INWARDS:
        parts.append(lax.ppermute(value, FAR, [(cube, 0)]))

    def total(extra):
        (*given, _) = lax.optimization_barrier((value, *parts, extra))
        whole = sum(part.astype(f32) for part in given).astype(bf16)
        whole = jnp.where(lax.axis_index(FAR) == 0, whole, jnp.zeros_like(whole))
        for steps in OUTWARDS:
            moved = []
            for pairs in steps:
                moved.append(lax.ppermute(whole, FAR, pairs))
            whole = sum(moved, whole)
        return whole

    return total


def call(kernel, outs, *operands, scratch=(), flops):
    in_vmem = pl.BlockSpec(memory_space=pltpu.VMEM)
    in_smem = pl.BlockSpec(memory_space=pltpu.SMEM)
    moved = sum(x.size * x.dtype.itemsize for x in (*operands, *outs))
    return pl.pallas_call(
        kernel,
        out_shape=outs,
        in_specs=[in_smem if x.dtype == jnp.int32 else in_vmem for x in operands],
        out_specs=tuple(in_vmem for _ in outs),
        scratch_shapes=list(scratch),
        compiler_params=pltpu.CompilerParams(vmem_limit_bytes=VMEM_BYTES),
        cost_estimate=pl.CostEstimate(flops=flops, bytes_accessed=moved, transcendentals=0),
    )(*operands)


def struct(shape, dtype):
    return jax.ShapeDtypeStruct(shape, dtype)


def over_tiles(width, body):
    def step(tile, carry):
        body(tile, pl.ds(pl.multiple_of(tile * LANES, LANES), LANES))
        return carry

    lax.fori_loop(0, width // LANES, step, 0)


def blocks(value):
    return [value[SUB * i : SUB * i + SUB] for i in range(value.shape[0] // SUB)]


def fill(window, at, value):
    window[pl.ds(at, value.shape[0]), :] = value.astype(f32)


def own_kernel(mixed, filters, conv, window):
    rows, width = mixed.shape
    count = rows // SUB
    window[pl.ds(0, SUB), :] = jnp.zeros((SUB, LANES), f32)

    def tile(_, lanes):
        fill(window, SUB, mixed[:, lanes])
        total = [None] * count
        for shift in range(SUB):
            slid = [window[pl.ds(SUB + SUB * i - shift, SUB), :] for i in range(count)]
            for step in range(count):
                weight = filters[pl.ds(SUB * step + shift, 1), lanes]
                for i in range(step, count):
                    term = weight * slid[i - step]
                    total[i] = term if total[i] is None else total[i] + term
        for i in range(count):
            conv[pl.ds(SUB * i, SUB), lanes] = total[i]

    over_tiles(width, tile)


def rim_kernel(own, earlier, filters, query, cot, gain, conv, sums, window, squares, crosses):
    rows, width = own.shape
    count = rows // SUB
    window[pl.ds(rows, SUB), :] = jnp.zeros((SUB, LANES), f32)
    squares[...] = jnp.zeros(squares.shape, f32)
    crosses[...] = jnp.zeros(crosses.shape, f32)

    def tile(_, lanes):
        fill(window, 0, earlier[:, lanes])
        total = [own[pl.ds(SUB * i, SUB), lanes] for i in range(count)]
        for shift in range(SUB):
            slid = [window[pl.ds(rows - SUB * i - shift, SUB), :] for i in range(count)]
            for step in range(count):
                weight = filters[pl.ds(SUB * step + shift, 1), lanes]
                for i in range(step + 1):
                    total[i] = total[i] + weight * slid[step - i]
        for i in range(count):
            at = pl.ds(SUB * i, SUB)
            conv[at, lanes] = total[i]
        whole = conv[:, lanes]
        product = query[:, lanes].astype(f32) * whole
        weighted = gain[:, lanes] * cot[:, lanes].astype(f32)
        squares[...] += product * product
        crosses[...] += weighted * product

    over_tiles(width, tile)
    square = jnp.sum(squares[...].T, 0, keepdims=True)
    cross = jnp.sum(crosses[...].T, 0, keepdims=True)
    first = lax.broadcasted_iota(jnp.int32, sums.shape[1:], 0) == 0
    both = jnp.where(first, square, cross)
    for i in range(sums.shape[0]):
        sums[i] = both


def gathered(parts):
    row = lax.broadcasted_iota(jnp.int32, (SUB, LANES), 0)
    half = 1
    while half < SUB:
        low = (row & half) == 0
        parts = [
            jnp.where(low, a, b) + pltpu.roll(jnp.where(low, b, a), half, 0)
            for a, b in zip(parts[::2], parts[1::2])
        ]
        half *= 2
    return parts[0]


def grads_kernel(
    sums, conv, query, cot, gain, earlier, mixed, grad_conv, grad_q, block, window, inverse, pull, partial
):
    rows, width = conv.shape
    count = rows // SUB
    both = jnp.sum(sums[...], 0)
    rms = jnp.sqrt(both[0:1] / D + epsilon)
    inverse[...] = jnp.broadcast_to(1.0 / rms, (LANES, rows)).T
    pull[...] = jnp.broadcast_to(both[1:2] / (D * (rms * rms * rms)), (LANES, rows)).T
    block[:, width:] = jnp.zeros((rows, LANES), bf16)

    def tile(index, lanes):
        whole = conv[:, lanes]
        query_f32 = query[:, lanes].astype(f32)
        cot_f32 = cot[:, lanes].astype(f32)
        product = query_f32 * whole
        grad_product = gain[:, lanes] * cot_f32 * inverse[...] - product * pull[...]
        rounded = (query_f32 * grad_product).astype(bf16)
        grad_conv[:, lanes] = rounded
        grad_q[:, lanes] = (grad_product * whole).astype(bf16)
        gains = jnp.sum((cot_f32 * product * inverse[...]).reshape(count, SUB, LANES), 0)
        block[pl.ds(pl.multiple_of(index * SUB, SUB), SUB), width:] = gains.astype(bf16)
        fill(window, 0, earlier[:, lanes])
        fill(window, rows, mixed[:, lanes])
        ours = blocks(rounded.astype(f32))
        for shift in range(SUB):
            slid = [window[pl.ds(SUB * (i + 1) - shift, SUB), :] for i in range(2 * count - 1)]
            for step in range(count):
                terms = [ours[i] * slid[count - 1 + i - step] for i in range(count)]
                while len(terms) > 1:
                    terms = [a + b for a, b in zip(terms[::2], terms[1::2])]
                partial[SUB * step + shift] = terms[0]
        for step in range(0, count, 2):
            pair = [gathered([partial[SUB * s + i] for i in range(SUB)]) for s in (step, step + 1)]
            block[pl.ds(SUB * step, 2 * SUB), lanes] = jnp.concatenate(pair, 0).astype(bf16)

    over_tiles(width, tile)


def back(grad_conv, later, filters, k_proj, v_proj, grad_k, grad_v, window):
    rows, width = grad_conv.shape
    count = rows // SUB

    def tile(_, lanes):
        fill(window, 0, grad_conv[:, lanes])
        fill(window, rows, later[:, lanes])
        total = [jnp.zeros((SUB, LANES), f32)] * count
        for shift in range(SUB):
            slid = [window[pl.ds(SUB * i + shift, SUB), :] for i in range(2 * count - 1)]
            for step in range(count):
                weight = filters[pl.ds(SUB * step + shift, 1), lanes]
                for i in range(count):
                    total[i] = total[i] + weight * slid[i + step]
        grad_mixed = jnp.concatenate(total, 0)
        grad_k[:, lanes] = (grad_mixed * v_proj[:, lanes].astype(f32)).astype(bf16)
        grad_v[:, lanes] = (grad_mixed * k_proj[:, lanes].astype(f32)).astype(bf16)

    over_tiles(width, tile)


def early_back_kernel(early, *refs):
    @pl.when(early[0] == 1)
    def _():
        back(*refs)


def late_back_kernel(early, early_k, early_v, *refs):
    grad_k, grad_v = refs[-3:-1]

    @pl.when(early[0] == 1)
    def _():
        grad_k[...] = early_k[...]
        grad_v[...] = early_v[...]

    @pl.when(early[0] == 0)
    def _():
        back(*refs)


def final_kernel(whole, grad_filters, grad_gain):
    width = grad_filters.shape[1]
    grad_filters[...] = whole[:, :width].astype(f32)
    for i in range(width // LANES):
        part = whole[pl.ds(SUB * i, SUB), width:].astype(f32)
        grad_gain[pl.ds(i, 1), :] = jnp.sum(part, 0, keepdims=True)


def device_part(q_proj, k_proj, v_proj, cotangent, filters, gain):
    rows, width = q_proj.shape
    macs = 2 * filters.shape[0] * rows * width
    tile = pltpu.VMEM((rows, LANES), f32)
    short = pltpu.VMEM((rows + SUB, LANES), f32)
    long = pltpu.VMEM((2 * rows, LANES), f32)
    gain = gain.reshape(1, width)
    mixed = (k_proj.astype(f32) * v_proj.astype(f32)).astype(bf16)
    earlier = passed_along(mixed, 1)
    (own,) = call(own_kernel, (struct((rows, width), f32),), mixed, filters, scratch=(short,), flops=macs // 2)
    members = lax.axis_size("tp")
    conv, sums = call(
        rim_kernel,
        (struct((rows, width), f32), struct((members, SUB, rows), f32)),
        own,
        earlier,
        filters,
        q_proj,
        cotangent,
        gain,
        scratch=(short, tile, tile),
        flops=macs // 2,
    )
    sums = lax.all_to_all(sums, "tp", 0, 0)
    grad_conv, grad_q, block = call(
        grads_kernel,
        (struct((rows, width), bf16), struct((rows, width), bf16), struct((rows, width + LANES), bf16)),
        sums,
        conv,
        q_proj,
        cotangent,
        gain,
        earlier,
        mixed,
        scratch=(long, tile, tile, pltpu.VMEM((rows, SUB, LANES), f32)),
        flops=macs,
    )
    near = lax.axis_size(NEAR)
    block = block.reshape(near, rows // near, width + LANES)
    block = lax.all_to_all(block, NEAR, 0, 0)
    block = jnp.sum(block.astype(f32), 0).astype(bf16)
    block, grad_conv = lax.optimization_barrier((block, grad_conv))
    total = far_sum(block)
    later = passed_along(grad_conv, -1)
    early = (lax.axis_index(FAR) < EARLY).astype(jnp.int32).reshape(1)
    grads = (struct((rows, width), bf16), struct((rows, width), bf16))
    sources = (grad_conv, later, filters, k_proj, v_proj)
    early_k, early_v = call(early_back_kernel, grads, early, *sources, scratch=(long,), flops=macs)
    whole = total(early_k)
    grad_k, grad_v = call(late_back_kernel, grads, early, early_k, early_v, *sources, scratch=(long,), flops=macs)
    whole, grad_k = lax.optimization_barrier((whole, grad_k))
    whole = shared(whole, NEAR).reshape(rows, width + LANES)
    grad_filters, grad_gain = call(
        final_kernel, (struct((rows, width), f32), struct((width // LANES, LANES), f32)), whole, flops=0
    )
    return (grad_q, grad_k, grad_v, grad_filters, grad_gain.reshape(width))


def solution(mesh):
    cube = 4
    far = mesh.devices.shape[0] // (cube * cube)
    split = Mesh(mesh.devices.reshape(far, cube, cube, -1), (*CTX, "tp"))
    rows = P(CTX, "tp")
    in_specs = (rows, rows, rows, rows, P(None, "tp"), P("tp"))
    out_specs = (rows, rows, rows, P(None, "tp"), P("tp"))
    return jax.shard_map(device_part, mesh=split, in_specs=in_specs, out_specs=out_specs, check_vma=False)
```

```python
import jax
import jax.numpy as jnp
from jax import lax
from jax.experimental import pallas as pl
from jax.experimental.pallas import tpu as pltpu
from jax.sharding import Mesh, PartitionSpec as P

D = 8192
CTX = ("zh", "zl", "x")
NEAR = ("zl", "x")
FAR = "zh"
INWARDS = (4, 5, 3, 2, 6, 1, 7)
OUTWARDS = (
    (((0, 1),), ((0, 7),)),
    (((7, 4), (1, 2)), ((7, 5),), ((7, 6),)),
    (((2, 3),),),
)
EARLY = 2
LANES = 128
SUB = 8
VMEM_BYTES = 8 << 20


epsilon = 1e-06
f32 = jnp.float32
bf16 = jnp.bfloat16


def passed_along(value, by):
    length = lax.axis_size(CTX)
    pairs = [(i, i + by) for i in range(length) if 0 <= i + by < length]
    return lax.ppermute(value, CTX, pairs)


def shared(value, axes):
    size = lax.axis_size(axes)
    copies = jnp.broadcast_to(value[None], (size, *value.shape))
    return lax.all_to_all(copies, axes, 0, 0)


def far_sum(value):
    assert lax.axis_size(FAR) == 1 + len(INWARDS)
    parts = []
    for cube in INWARDS:
        parts.append(lax.ppermute(value, FAR, [(cube, 0)]))

    def total(extra):
        (*given, _) = lax.optimization_barrier((value, *parts, extra))
        whole = sum(part.astype(f32) for part in given).astype(bf16)
        whole = jnp.where(lax.axis_index(FAR) == 0, whole, jnp.zeros_like(whole))
        for steps in OUTWARDS:
            moved = []
            for pairs in steps:
                moved.append(lax.ppermute(whole, FAR, pairs))
            whole = sum(moved, whole)
        return whole

    return total


def call(kernel, outs, *operands, scratch=(), flops):
    in_vmem = pl.BlockSpec(memory_space=pltpu.VMEM)
    in_smem = pl.BlockSpec(memory_space=pltpu.SMEM)
    moved = sum(x.size * x.dtype.itemsize for x in (*operands, *outs))
    return pl.pallas_call(
        kernel,
        out_shape=outs,
        in_specs=[in_smem if x.dtype == jnp.int32 else in_vmem for x in operands],
        out_specs=tuple(in_vmem for _ in outs),
        scratch_shapes=list(scratch),
        compiler_params=pltpu.CompilerParams(vmem_limit_bytes=VMEM_BYTES),
        cost_estimate=pl.CostEstimate(flops=flops, bytes_accessed=moved, transcendentals=0),
    )(*operands)


def struct(shape, dtype):
    return jax.ShapeDtypeStruct(shape, dtype)


def over_tiles(width, body):
    def step(tile, carry):
        body(tile, pl.ds(pl.multiple_of(tile * LANES, LANES), LANES))
        return carry

    lax.fori_loop(0, width // LANES, step, 0)


def blocks(value):
    return [value[SUB * i : SUB * i + SUB] for i in range(value.shape[0] // SUB)]


def fill(window, at, value):
    window[pl.ds(at, value.shape[0]), :] = value.astype(f32)


def own_kernel(mixed, filters, conv, window):
    rows, width = mixed.shape
    count = rows // SUB
    window[pl.ds(0, SUB), :] = jnp.zeros((SUB, LANES), f32)

    def tile(_, lanes):
        fill(window, SUB, mixed[:, lanes])
        total = [None] * count
        for shift in range(SUB):
            slid = [window[pl.ds(SUB + SUB * i - shift, SUB), :] for i in range(count)]
            for step in range(count):
                weight = filters[pl.ds(SUB * step + shift, 1), lanes]
                for i in range(step, count):
                    term = weight * slid[i - step]
                    total[i] = term if total[i] is None else total[i] + term
        for i in range(count):
            conv[pl.ds(SUB * i, SUB), lanes] = total[i]

    over_tiles(width, tile)


def rim_kernel(own, earlier, filters, query, cot, gain, conv, sums, window, squares, crosses):
    rows, width = own.shape
    count = rows // SUB
    window[pl.ds(rows, SUB), :] = jnp.zeros((SUB, LANES), f32)
    squares[...] = jnp.zeros(squares.shape, f32)
    crosses[...] = jnp.zeros(crosses.shape, f32)

    def tile(_, lanes):
        fill(window, 0, earlier[:, lanes])
        total = [own[pl.ds(SUB * i, SUB), lanes] for i in range(count)]
        for shift in range(SUB):
            slid = [window[pl.ds(rows - SUB * i - shift, SUB), :] for i in range(count)]
            for step in range(count):
                weight = filters[pl.ds(SUB * step + shift, 1), lanes]
                for i in range(step + 1):
                    total[i] = total[i] + weight * slid[step - i]
        for i in range(count):
            at = pl.ds(SUB * i, SUB)
            conv[at, lanes] = total[i]
        whole = conv[:, lanes]
        product = query[:, lanes].astype(f32) * whole
        weighted = gain[:, lanes] * cot[:, lanes].astype(f32)
        squares[...] += product * product
        crosses[...] += weighted * product

    over_tiles(width, tile)
    square = jnp.sum(squares[...].T, 0, keepdims=True)
    cross = jnp.sum(crosses[...].T, 0, keepdims=True)
    first = lax.broadcasted_iota(jnp.int32, sums.shape[1:], 0) == 0
    both = jnp.where(first, square, cross)
    for i in range(sums.shape[0]):
        sums[i] = both


def gathered(parts):
    row = lax.broadcasted_iota(jnp.int32, (SUB, LANES), 0)
    half = 1
    while half < SUB:
        low = (row & half) == 0
        parts = [
            jnp.where(low, a, b) + pltpu.roll(jnp.where(low, b, a), half, 0)
            for a, b in zip(parts[::2], parts[1::2])
        ]
        half *= 2
    return parts[0]


def grads_kernel(
    sums, conv, query, cot, gain, earlier, mixed, grad_conv, grad_q, block, window, inverse, pull, partial
):
    rows, width = conv.shape
    count = rows // SUB
    both = jnp.sum(sums[...], 0)
    rms = jnp.sqrt(both[0:1] / D + epsilon)
    inverse[...] = jnp.broadcast_to(1.0 / rms, (LANES, rows)).T
    pull[...] = jnp.broadcast_to(both[1:2] / (D * (rms * rms * rms)), (LANES, rows)).T
    block[:, width:] = jnp.zeros((rows, LANES), bf16)

    def tile(index, lanes):
        whole = conv[:, lanes]
        query_f32 = query[:, lanes].astype(f32)
        cot_f32 = cot[:, lanes].astype(f32)
        product = query_f32 * whole
        grad_product = gain[:, lanes] * cot_f32 * inverse[...] - product * pull[...]
        rounded = (query_f32 * grad_product).astype(bf16)
        grad_conv[:, lanes] = rounded
        grad_q[:, lanes] = (grad_product * whole).astype(bf16)
        gains = jnp.sum((cot_f32 * product * inverse[...]).reshape(count, SUB, LANES), 0)
        block[pl.ds(pl.multiple_of(index * SUB, SUB), SUB), width:] = gains.astype(bf16)
        fill(window, 0, earlier[:, lanes])
        fill(window, rows, mixed[:, lanes])
        ours = blocks(rounded.astype(f32))
        for shift in range(SUB):
            slid = [window[pl.ds(SUB * (i + 1) - shift, SUB), :] for i in range(2 * count - 1)]
            for step in range(count):
                terms = [ours[i] * slid[count - 1 + i - step] for i in range(count)]
                while len(terms) > 1:
                    terms = [a + b for a, b in zip(terms[::2], terms[1::2])]
                partial[SUB * step + shift] = terms[0]
        for step in range(0, count, 2):
            pair = [gathered([partial[SUB * s + i] for i in range(SUB)]) for s in (step, step + 1)]
            block[pl.ds(SUB * step, 2 * SUB), lanes] = jnp.concatenate(pair, 0).astype(bf16)

    over_tiles(width, tile)


def back(grad_conv, later, filters, k_proj, v_proj, grad_k, grad_v, window):
    rows, width = grad_conv.shape
    count = rows // SUB

    def tile(_, lanes):
        fill(window, 0, grad_conv[:, lanes])
        fill(window, rows, later[:, lanes])
        total = [jnp.zeros((SUB, LANES), f32)] * count
        for shift in range(SUB):
            slid = [window[pl.ds(SUB * i + shift, SUB), :] for i in range(2 * count - 1)]
            for step in range(count):
                weight = filters[pl.ds(SUB * step + shift, 1), lanes]
                for i in range(count):
                    total[i] = total[i] + weight * slid[i + step]
        grad_mixed = jnp.concatenate(total, 0)
        grad_k[:, lanes] = (grad_mixed * v_proj[:, lanes].astype(f32)).astype(bf16)
        grad_v[:, lanes] = (grad_mixed * k_proj[:, lanes].astype(f32)).astype(bf16)

    over_tiles(width, tile)


def early_back_kernel(early, *refs):
    @pl.when(early[0] == 1)
    def _():
        back(*refs)


def late_back_kernel(early, early_k, early_v, *refs):
    grad_k, grad_v = refs[-3:-1]

    @pl.when(early[0] == 1)
    def _():
        grad_k[...] = early_k[...]
        grad_v[...] = early_v[...]

    @pl.when(early[0] == 0)
    def _():
        back(*refs)


def final_kernel(whole, grad_filters, grad_gain):
    width = grad_filters.shape[1]
    grad_filters[...] = whole[:, :width].astype(f32)
    for i in range(width // LANES):
        part = whole[pl.ds(SUB * i, SUB), width:].astype(f32)
        grad_gain[pl.ds(i, 1), :] = jnp.sum(part, 0, keepdims=True)


def device_part(q_proj, k_proj, v_proj, cotangent, filters, gain):
    rows, width = q_proj.shape
    macs = 2 * filters.shape[0] * rows * width
    tile = pltpu.VMEM((rows, LANES), f32)
    short = pltpu.VMEM((rows + SUB, LANES), f32)
    long = pltpu.VMEM((2 * rows, LANES), f32)
    gain = gain.reshape(1, width)
    mixed = (k_proj.astype(f32) * v_proj.astype(f32)).astype(bf16)
    earlier = passed_along(mixed, 1)
    (own,) = call(own_kernel, (struct((rows, width), f32),), mixed, filters, scratch=(short,), flops=macs // 2)
    members = lax.axis_size("tp")
    conv, sums = call(
        rim_kernel,
        (struct((rows, width), f32), struct((members, SUB, rows), f32)),
        own,
        earlier,
        filters,
        q_proj,
        cotangent,
        gain,
        scratch=(short, tile, tile),
        flops=macs // 2,
    )
    sums = lax.all_to_all(sums, "tp", 0, 0)
    grad_conv, grad_q, block = call(
        grads_kernel,
        (struct((rows, width), bf16), struct((rows, width), bf16), struct((rows, width + LANES), bf16)),
        sums,
        conv,
        q_proj,
        cotangent,
        gain,
        earlier,
        mixed,
        scratch=(long, tile, tile, pltpu.VMEM((rows, SUB, LANES), f32)),
        flops=macs,
    )
    near = lax.axis_size(NEAR)
    block = block.reshape(near, rows // near, width + LANES)
    block = lax.all_to_all(block, NEAR, 0, 0)
    block = jnp.sum(block.astype(f32), 0).astype(bf16)
    block, grad_conv = lax.optimization_barrier((block, grad_conv))
    total = far_sum(block)
    later = passed_along(grad_conv, -1)
    early = (lax.axis_index(FAR) < EARLY).astype(jnp.int32).reshape(1)
    grads = (struct((rows, width), bf16), struct((rows, width), bf16))
    sources = (grad_conv, later, filters, k_proj, v_proj)
    early_k, early_v = call(early_back_kernel, grads, early, *sources, scratch=(long,), flops=macs)
    whole = total(early_k)
    grad_k, grad_v = call(late_back_kernel, grads, early, early_k, early_v, *sources, scratch=(long,), flops=macs)
    whole, grad_k = lax.optimization_barrier((whole, grad_k))
    whole = shared(whole, NEAR).reshape(rows, width + LANES)
    grad_filters, grad_gain = call(
        final_kernel, (struct((rows, width), f32), struct((width // LANES, LANES), f32)), whole, flops=0
    )
    return (grad_q, grad_k, grad_v, grad_filters, grad_gain.reshape(width))


def solution(mesh):
    cube = 4
    far = mesh.devices.shape[0] // (cube * cube)
    split = Mesh(mesh.devices.reshape(far, cube, cube, -1), (*CTX, "tp"))
    rows = P(CTX, "tp")
    in_specs = (rows, rows, rows, rows, P(None, "tp"), P("tp"))
    out_specs = (rows, rows, rows, P(None, "tp"), P("tp"))
    return jax.shard_map(device_part, mesh=split, in_specs=in_specs, out_specs=out_specs, check_vma=False)
```
